512 devices in a mesh: depth: 8 (over y, core), lon: 64 (over x, z).
Axes of the slice: x: 4, y: 4, z: 16, core: 2. Of those that a mesh axis runs over, the one named last changes fastest.
Arguments:
- probes: float32 [16, 1179648], P(None, ('depth', 'lon'))
- coords: float32 [3, 1179648], P(None, ('depth', 'lon')), as said below
- pair_tiles: int32 [2, 57344], P(None, ('depth', 'lon')), may hold values from 0 to 42, as said below
- scales: float32 [2], replicated, may hold values from 0.5 to 2
Outputs:
- solution: float32 [16, 1179648], P(None, ('depth', 'lon'))
- residual: float32 [16, 1179648], P(None, ('depth', 'lon'))
The draws below stay inside these ranges and needn't reach their ends.
Inputs may be any that keep to these rules, and one draw needn't show every extreme that they name: `pair_tiles`: row 0 holds row tiles 0 to 8 of the device holding the entry, used slots first, then 9 in every unused slot. Row 1 holds codes s * 9 + t of tile t of the same device (s = 0), of the device one lower (1) or one higher (2) along lon, one lower (3) or one higher (4) along depth; codes with s = 1 have t >= 7, codes with s = 2 have t < 2, codes with s = 3 or 4 have 2 <= t < 7; no code points past an edge of the mesh; unused slots hold code 0. `coords`: two points closer than 1 always lie in tiles that form a used pair.
All inputs are finite; a program needn't handle non-finite values.
Results may differ from the reference program's by a relative error of at most 0.0003.
Values sent between devices are 32-bit elements; how exact they have to be, the bound alone decides.
No kernel may reach another device: no remote copies, remote signals or barrier semaphores. Data moves between devices by JAX's collectives and lax.ppermute only.
A program may use at most 64 MiB of HBM per device.

```python
import math
import jax
import jax.numpy as jnp
from jax import lax

PROBES = 16
TILE = 256
TD = 9
BT = 2
CW = 6
ITERS = 2
PAIRS_DEV = 112
NTILES = 4608
NPTS = 1179648
N_DEPTH = 8
N_LON = 64
DEVICES = 512


def tile_layout(key):
    spread_key, pick_key = jax.random.split(jax.random.fold_in(key, 11))
    spread = jax.random.randint(spread_key, (N_DEPTH, N_LON, 1), 1, CW - 1)
    first_lon = jnp.arange(N_LON, dtype=jnp.int32)[None, :, None] == 0
    spread = jnp.where(first_lon, 1, spread)
    picks = jax.random.randint(pick_key, (N_DEPTH, N_LON, TD - 2 * BT), 0, 1 << 20) % spread
    middle = 1 + jnp.sort(picks, axis=-1)
    return jnp.concatenate([jnp.zeros((N_DEPTH, N_LON, BT), jnp.int32), middle.astype(jnp.int32), jnp.full((N_DEPTH, N_LON, BT), CW - 1, jnp.int32)], axis=-1)


def draw_pair_tiles(key, part):
    tile_cells = tile_layout(key)
    tile_ids = jnp.arange(TD, dtype=jnp.int32)
    interior = (tile_ids >= BT) & (tile_ids < TD - BT)
    lon_ids = jnp.arange(N_LON, dtype=jnp.int32)[None, :, None, None]
    depth_ids = jnp.arange(N_DEPTH, dtype=jnp.int32)[:, None, None, None]
    row_grid = jnp.broadcast_to(tile_ids[:, None], (TD, TD)).reshape(TD * TD)
    col_grid = jnp.broadcast_to(tile_ids[None, :], (TD, TD)).reshape(TD * TD)
    below_cells = jnp.concatenate([tile_cells[:1], tile_cells[:-1]], axis=0)
    above_cells = jnp.concatenate([tile_cells[1:], tile_cells[-1:]], axis=0)
    pair_inner = interior[:, None] & interior[None, :]

    def close_pairs(near_cells, far_cells, allowed):
        close = jnp.abs(near_cells[..., :, None] - far_cells[..., None, :]) <= 1
        return jnp.broadcast_to(close & allowed, (N_DEPTH, N_LON, TD, TD)).reshape(N_DEPTH, N_LON, TD * TD)
    left_allow = (tile_ids[:, None] < BT) & (tile_ids[None, :] >= TD - BT) & (lon_ids > 0)
    right_allow = (tile_ids[:, None] >= TD - BT) & (tile_ids[None, :] < BT) & (lon_ids < N_LON - 1)
    own_ok = close_pairs(tile_cells, tile_cells, True)
    left_ok = jnp.broadcast_to(left_allow, (N_DEPTH, N_LON, TD, TD)).reshape(N_DEPTH, N_LON, TD * TD)
    right_ok = jnp.broadcast_to(right_allow, (N_DEPTH, N_LON, TD, TD)).reshape(N_DEPTH, N_LON, TD * TD)
    below_ok = close_pairs(tile_cells, below_cells, pair_inner & (depth_ids > 0))
    above_ok = close_pairs(tile_cells, above_cells, pair_inner & (depth_ids < N_DEPTH - 1))
    valid = jnp.concatenate([own_ok, left_ok, right_ok, below_ok, above_ok], axis=-1)
    rows_all = jnp.tile(row_grid, 5)
    codes_all = jnp.concatenate([source_id * TD + col_grid for source_id in range(5)])
    rows_all = jnp.where(valid, rows_all, TD)
    codes_all = jnp.where(valid, codes_all, 0)
    order = jnp.argsort(jnp.where(valid, 0, 1).astype(jnp.int32), axis=-1, stable=True)[..., :PAIRS_DEV]
    row_pick = jnp.take_along_axis(rows_all, order, axis=-1)
    code_pick = jnp.take_along_axis(codes_all, order, axis=-1)
    return jnp.stack([row_pick.reshape(-1), code_pick.reshape(-1)]).astype(jnp.int32)


def draw_coords(key, part):
    tile_cells = tile_layout(key).astype(jnp.float32)
    spots = jax.random.uniform(jax.random.fold_in(key, 23), (3, N_DEPTH, N_LON, TD, TILE), jnp.float32)
    tile_ids = jnp.arange(TD, dtype=jnp.int32)
    interior = ((tile_ids >= BT) & (tile_ids < TD - BT))[None, None, :, None]
    lon_base = (jnp.arange(N_LON, dtype=jnp.float32) * CW)[None, :, None, None]
    depth_base = (2.0 * jnp.arange(N_DEPTH, dtype=jnp.float32))[:, None, None, None]
    east = lon_base + tile_cells[..., None] + spots[0]
    down = jnp.where(interior, depth_base + 2.0 * spots[1], depth_base + 1.0 + 0.0 * spots[1])
    north = 16.0 * spots[2]
    return jnp.stack([east, down, north]).reshape(3, NPTS).astype(jnp.float32)


def draw_probes(key, part):
    values = jax.random.truncated_normal(jax.random.fold_in(key, 31), -6.0, 6.0, (PROBES, DEVICES, TD * TILE), jnp.float32)
    rising = 1.0 + 2.0 * jnp.arange(DEVICES, dtype=jnp.float32) / (DEVICES - 1)
    return (values * rising[None, :, None]).reshape(PROBES, NPTS).astype(jnp.float32)


def setup_inputs(seed: int = 0) -> dict:
    splits = jax.random.split(jax.random.key(seed), 5)
    probes = draw_probes(jax.random.fold_in(splits[4], 71), 0)
    coords = draw_coords(jax.random.fold_in(splits[4], 71), 0)
    pair_tiles = draw_pair_tiles(jax.random.fold_in(splits[4], 71), 0)
    scales = jnp.clip(jnp.exp(jax.random.uniform(splits[3], (2,), jnp.float32, math.log(0.5), math.log(2.0))), 0.5, 2.0)
    return dict(probes=probes, coords=coords, pair_tiles=pair_tiles, scales=scales)


def kernel_tile(near_pts, far_pts):
    dist_sq = (near_pts[0][:, :, None] - far_pts[0][:, None, :]) ** 2
    dist_sq = dist_sq + (near_pts[1][:, :, None] - far_pts[1][:, None, :]) ** 2
    dist_sq = dist_sq + (near_pts[2][:, :, None] - far_pts[2][:, None, :]) ** 2
    radius = jnp.sqrt(dist_sq)
    inside = jnp.maximum(1.0 - radius, 0.0)
    return inside ** 4 * (4.0 * radius + 1.0)

def inner_product(first_arr, second_arr):
    return lax.optimization_barrier(jnp.sum(first_arr * second_arr, axis=(1, 2)))

def reference(probes, coords, pair_tiles, scales):
    row_tiles = pair_tiles[0]
    col_codes = pair_tiles[1]
    owner_dev = jnp.arange(DEVICES * PAIRS_DEV, dtype=jnp.int32) // PAIRS_DEV
    source = col_codes // TD
    within = col_codes % TD
    moves = jnp.array([0, -1, 1, -N_LON, N_LON], dtype=jnp.int32)
    near_glob = jnp.where(row_tiles < TD, owner_dev * TD + row_tiles, NTILES).astype(jnp.int32)
    far_glob = jnp.clip((owner_dev + moves[source]) * TD + within, 0, NTILES - 1).astype(jnp.int32)
    near_blocks = near_glob.reshape(-1, 16)
    far_blocks = far_glob.reshape(-1, 16)
    points = coords.reshape(3, NTILES, TILE)

    def operate(vectors):

        def add_block(running, pair_idx):
            near_rows, far_rows = pair_idx
            near_pts = points[:, jnp.minimum(near_rows, NTILES - 1)]
            far_pts = points[:, far_rows]
            weights = kernel_tile(near_pts, far_pts)
            contrib = jnp.einsum('pij,cpj->cpi', weights, vectors[:, far_rows], precision=lax.Precision.HIGHEST)
            return (running.at[:, near_rows].add(contrib, mode='drop'), None)
        running, _ = lax.scan(add_block, jnp.zeros(vectors.shape, jnp.float32), (near_blocks, far_blocks))
        return scales[1] * vectors + scales[0] * running
    residual = probes.reshape(PROBES, NTILES, TILE)
    direction = residual
    solution = jnp.zeros(residual.shape, jnp.float32)
    norm_now = inner_product(residual, residual)
    for sweep_index in range(ITERS):
        applied = operate(direction)
        step_size = norm_now / inner_product(direction, applied)
        solution = solution + step_size[:, None, None] * direction
        residual = residual - step_size[:, None, None] * applied
        norm_next = inner_product(residual, residual)
        direction = residual + (norm_next / norm_now)[:, None, None] * direction
        norm_now = norm_next
    return (solution.reshape(PROBES, NPTS), residual.reshape(PROBES, NPTS))
```

```python
import jax
import jax.numpy as jnp
from jax import lax
from jax.experimental import pallas as pl
from jax.experimental.pallas import tpu as pltpu
from jax.sharding import Mesh, PartitionSpec as P

PROBES = 16
TILE = 256
TD = 9
BT = 2
MID = TD - 2 * BT
HALO = 2 * BT + 2 * MID
CHUNK = 32
ROWS = 24
FIRST = ROWS - PROBES
VMEM = pltpu.MemorySpace.VMEM
SMEM = pltpu.MemorySpace.SMEM
PARTS = ((0, BT), (BT, MID), (TD - BT, BT))


def call(kernel, out_shape, in_specs, scratch=(), aliases=None, flops=0, nbytes=0, limit=20):
    return pl.pallas_call(
        kernel,
        out_shape=out_shape,
        in_specs=in_specs,
        out_specs=jax.tree.map(lambda _: pl.BlockSpec(memory_space=VMEM), out_shape),
        scratch_shapes=scratch,
        input_output_aliases=aliases or {},
        compiler_params=pltpu.CompilerParams(vmem_limit_bytes=limit << 20),
        cost_estimate=pl.CostEstimate(flops=flops, bytes_accessed=nbytes, transcendentals=0),
    )


def spec(space=VMEM):
    return pl.BlockSpec(memory_space=space)


def f32(*shape):
    return jax.ShapeDtypeStruct(shape, jnp.float32)


def pack_kernel(probes, coords, left, mid, right):
    for (first, count), out in zip(PARTS, (left, mid, right)):
        cols = pl.ds(first * TILE, count * TILE)
        out[0:FIRST, :] = jnp.zeros((FIRST, count * TILE), jnp.float32)
        out[0:3, :] = coords[:, cols]
        out[FIRST:ROWS, :] = probes[:, cols]


def make_lists(pairs, slots, own, rows, cols):
    def step(j, counts):
        taken, inside = counts
        row, code = pairs[0, j], pairs[1, j]
        used = row < TD
        local = used & (code < TD)
        source = code // TD
        tile = code - source * TD
        if own:
            keep, place = local, tile
        else:
            keep = used & (code >= TD)
            place = jnp.where(
                source == 1,
                tile - (TD - BT),
                jnp.where(source == 2, tile + BT, tile + BT + jnp.where(source == 3, 0, MID)),
            )
        rows[taken] = row
        cols[taken] = place
        return taken + keep.astype(jnp.int32), inside + local.astype(jnp.int32)

    taken, inside = lax.fori_loop(0, slots, step, (0, 0))
    rows[taken] = 0
    cols[taken] = 0
    return taken, inside


def split(values):
    high = values.astype(jnp.bfloat16)
    return high, (values - high.astype(jnp.float32)).astype(jnp.bfloat16)


def put_vectors(values, vecs, at):
    high, low = split(values)
    vecs[at, 0:PROBES, :] = high
    vecs[at, PROBES:, :] = low


def evaluate(near, far, slot, high, low):
    x, y, z = near[0:1, :], near[1:2, :], near[2:3, :]
    for first in range(0, TILE, CHUNK):
        rows = pl.ds(first, CHUNK)
        dx = far[rows, 0:1] - x
        dy = far[rows, 1:2] - y
        dz = far[rows, 2:3] - z
        dist_sq = dx * dx + dy * dy + dz * dz
        radius = dist_sq * lax.rsqrt(jnp.maximum(dist_sq, 1e-30))
        inside = jnp.maximum(1.0 - radius, 0.0)
        square = inside * inside
        phi = (square * square) * (1.25 - inside)
        top, rest = split(phi)
        high[slot, rows, :] = top
        low[slot, rows, :] = rest


def multiply(vecs, source, slot, high, low):
    both = jnp.dot(vecs[source], high[slot], preferred_element_type=jnp.float32)
    rest = jnp.dot(vecs[source, 0:PROBES, :], low[slot], preferred_element_type=jnp.float32)
    return both[0:PROBES] + both[PROBES:] + rest


def first_sweep(base, taken, rows, cols, near, far, vecs, total, high, low):
    def phi(k):
        evaluate(near.at[rows[k]], far.at[cols[k]], base + k, high, low)

    @pl.when(taken > 0)
    def _():
        phi(0)

    def step(k, carry):
        a, b = rows[k - 1], cols[k - 1]
        total[a] += multiply(vecs, b, base + k - 1, high, low)
        phi(k)
        return carry

    lax.fori_loop(1, taken + 1, step, 0)


def second_sweep(base, taken, rows, cols, vecs, total, high, low):
    def step(k, carry):
        a, b = rows[k], cols[k]
        total[a] += multiply(vecs, b, base + k, high, low)
        return carry

    lax.fori_loop(0, taken, step, 0)


def own_blocks(refs):
    for (first, count), ref in zip(PARTS, refs):
        for t in range(count):
            yield first + t, ref, pl.ds(t * TILE, TILE)


def halo_blocks(from_left, from_right, below, above):
    at = 0
    for ref, count in ((from_left, BT), (from_right, BT), (below, MID), (above, MID)):
        for t in range(count):
            yield at, ref, pl.ds(t * TILE, TILE)
            at += 1


def phi_own_kernel(pairs, left, mid, right, total, high, low, rows, cols, near, far, vecs):
    taken, _ = make_lists(pairs, pairs.shape[1], True, rows, cols)
    for t, ref, at in own_blocks((left, mid, right)):
        near[t] = ref[0:FIRST, at]
        far[t] = ref[0:FIRST, at].T
        put_vectors(ref[FIRST:ROWS, at], vecs, t)
    total[...] = jnp.zeros_like(total)
    first_sweep(0, taken, rows, cols, near, far, vecs, total, high, low)


def phi_halo_kernel(
    pairs, scales, left, mid, right, from_left, from_right, below, above, part, high_in, low_in,
    p_left, p_mid, p_right, high, low, rows, cols, near, far, vecs, total,
):
    taken, base = make_lists(pairs, pairs.shape[1], False, rows, cols)
    for t, ref, at in own_blocks((left, mid, right)):
        near[t] = ref[0:FIRST, at]
    for t, ref, at in halo_blocks(from_left, from_right, below, above):
        far[t] = ref[0:FIRST, at].T
        put_vectors(ref[FIRST:ROWS, at], vecs, t)
    total[...] = part[...]
    first_sweep(base, taken, rows, cols, near, far, vecs, total, high, low)
    outs = {}
    for t, ref, at in own_blocks((p_left, p_mid, p_right)):
        outs[t] = (ref, at)
    for t, ref, at in own_blocks((left, mid, right)):
        out, place = outs[t]
        out[:, place] = scales[0] * (4.0 * total[t] - ref[FIRST:ROWS, at])


def own_kernel(pairs, left, mid, right, high, low, total, rows, cols, vecs):
    taken, _ = make_lists(pairs, pairs.shape[1], True, rows, cols)
    for t, ref, at in own_blocks((left, mid, right)):
        put_vectors(ref[:, at], vecs, t)
    total[...] = jnp.zeros_like(total)
    second_sweep(0, taken, rows, cols, vecs, total, high, low)


def halo_kernel(
    pairs, scales, probes, left, mid, right, from_left, from_right, below, above, part, high, low,
    image, dots, rows, cols, vecs, total,
):
    taken, base = make_lists(pairs, pairs.shape[1], False, rows, cols)
    for t, ref, at in halo_blocks(from_left, from_right, below, above):
        put_vectors(ref[:, at], vecs, t)
    total[...] = part[...]
    second_sweep(base, taken, rows, cols, vecs, total, high, low)
    sums = [jnp.zeros((PROBES, TILE), jnp.float32) for _ in range(5)]
    for t, ref, at in own_blocks((left, mid, right)):
        p = ref[:, at]
        u = scales[0] * (4.0 * total[t] - p)
        r = probes[:, pl.ds(t * TILE, TILE)]
        image[:, pl.ds(t * TILE, TILE)] = u
        for i, (one, other) in enumerate(((r, r), (r, p), (p, p), (r, u), (p, u))):
            sums[i] = sums[i] + one * other
    lane = lax.broadcasted_iota(jnp.int32, (PROBES, 128), 1)
    probe = lax.broadcasted_iota(jnp.int32, (PROBES, 128), 0)
    line = jnp.zeros((PROBES, 128), jnp.float32)
    for i, value in enumerate(sums):
        line = line + jnp.where(lane == i * PROBES + probe, jnp.sum(value, axis=1, keepdims=True), 0.0)
    dots[...] = jnp.broadcast_to(jnp.sum(line, axis=0, keepdims=True), dots.shape)


def pass_kernel(gathered, out):
    out[...] = jnp.broadcast_to(jnp.sum(gathered[...], axis=0, keepdims=True), out.shape)


def final_kernel(gathered, scales, probes, left, mid, right, image, solution, residual):
    line = jnp.sum(gathered[...], axis=0, keepdims=True)
    lane = lax.broadcasted_iota(jnp.int32, (PROBES, 128), 1)
    probe = lax.broadcasted_iota(jnp.int32, (PROBES, 128), 0)
    spread = jnp.broadcast_to(line, (PROBES, 128))
    rr, rp, pp, ru, pu = [
        jnp.sum(jnp.where(lane == i * PROBES + probe, spread, 0.0), axis=1, keepdims=True)
        for i in range(5)
    ]
    shift = scales[0] + scales[1]
    first = rr / (shift * rr + rp)
    ratio = rp / rr
    norm = first * first * (pp - rp * ratio)
    turn = norm / rr
    keep = first * ratio + turn
    curve = (
        shift * (norm + turn * norm) + keep * keep * rp - keep * first * (ru + pp) + first * first * pu
    )
    second = norm / curve
    own_r = first + second * keep
    own_p = second * first
    res_r = first * ratio - second * shift * keep
    res_p = second * (shift * first - keep) - first
    res_u = second * first
    for t, ref, at in own_blocks((left, mid, right)):
        cols = pl.ds(t * TILE, TILE)
        r, p = probes[:, cols], ref[:, at]
        solution[:, cols] = own_r * r - own_p * p
        residual[:, cols] = res_r * r + res_p * p + res_u * image[:, cols]


def body(probes, coords, pairs, scales):
    slots = pairs.shape[1]
    width = probes.shape[1]
    lists = [pltpu.SMEM((slots + 1,), jnp.int32), pltpu.SMEM((slots + 1,), jnp.int32)]
    pair_flops = 40 * TILE * TILE * slots // 2
    stored = (slots + 1, TILE, TILE)
    kept = (pltpu.VMEM(stored, jnp.bfloat16), pltpu.VMEM(stored, jnp.bfloat16))
    pieces = lambda rows: tuple(f32(rows, count * TILE) for _, count in PARTS)

    def exchange(left, mid, right):
        lon = ("x", "z")
        depth = ("y", "core")
        up = lambda axes: [(i, i + 1) for i in range(lax.axis_size(axes) - 1)]
        down = lambda axes: [(i + 1, i) for i in range(lax.axis_size(axes) - 1)]
        return (
            lax.ppermute(right, lon, up(lon)),
            lax.ppermute(left, lon, down(lon)),
            lax.ppermute(mid, depth, up(depth)),
            lax.ppermute(mid, depth, down(depth)),
        )

    def pinned(*arrays):
        return tuple(pltpu.with_memory_space_constraint(a, VMEM) for a in arrays)

    packed = call(pack_kernel, pieces(ROWS), [spec()] * 2, nbytes=8 * ROWS * width)(probes, coords)
    halo = exchange(*packed)
    part, high, low = call(
        phi_own_kernel,
        (f32(TD, PROBES, TILE), *kept),
        [spec(SMEM)] + [spec()] * 3,
        scratch=[
            *lists,
            pltpu.VMEM((TD, FIRST, TILE), jnp.float32),
            pltpu.VMEM((TD, TILE, FIRST), jnp.float32),
            pltpu.VMEM((TD, 2 * PROBES, TILE), jnp.bfloat16),
        ],
        flops=pair_flops,
        nbytes=1 << 20,
    )(pairs, *packed)
    *image, high, low = call(
        phi_halo_kernel,
        (*pieces(PROBES), *kept),
        [spec(SMEM)] * 2 + [spec()] * 10,
        scratch=[
            *lists,
            pltpu.VMEM((TD, FIRST, TILE), jnp.float32),
            pltpu.VMEM((HALO, TILE, FIRST), jnp.float32),
            pltpu.VMEM((HALO, 2 * PROBES, TILE), jnp.bfloat16),
            pltpu.VMEM((TD, PROBES, TILE), jnp.float32),
        ],
        aliases={10: 3, 11: 4},
        flops=pair_flops,
        nbytes=1 << 20,
    )(pairs, scales, *packed, *halo, part, *pinned(high, low))
    halo = exchange(*image)
    part = call(
        own_kernel,
        f32(TD, PROBES, TILE),
        [spec(SMEM)] + [spec()] * 5,
        scratch=[*lists, pltpu.VMEM((TD, 2 * PROBES, TILE), jnp.bfloat16)],
        flops=pair_flops // 2,
        nbytes=1 << 20,
    )(pairs, *image, *pinned(high, low))
    far_image, dots = call(
        halo_kernel,
        (f32(PROBES, width), f32(lax.axis_size(("core", "z")), 128)),
        [spec(SMEM)] * 2 + [spec()] * 11,
        scratch=[
            *lists,
            pltpu.VMEM((HALO, 2 * PROBES, TILE), jnp.bfloat16),
            pltpu.VMEM((TD, PROBES, TILE), jnp.float32),
        ],
        flops=pair_flops // 2,
        nbytes=1 << 20,
    )(pairs, scales, probes, *image, *halo, part, *pinned(high, low))

    def swap(rows, axes):
        return lax.all_to_all(rows[:, None, :], axes, 0, 0, tiled=True)[:, 0, :]

    rows = swap(dots, ("core", "z"))
    rows = call(pass_kernel, f32(lax.axis_size(("y", "x")), 128), [spec()])(rows)
    rows = swap(rows, ("y", "x"))
    return call(final_kernel, (f32(PROBES, width),) * 2, [spec(), spec(SMEM)] + [spec()] * 5)(
        rows, scales, probes, *image, far_image
    )


def solution(mesh):
    shape = mesh.devices.shape
    cut = Mesh(mesh.devices.reshape(shape[0] // 2, 2, 4, shape[1] // 4), ("y", "core", "x", "z"))
    whole = ("y", "core", "x", "z")
    return jax.shard_map(
        body,
        mesh=cut,
        in_specs=(P(None, whole), P(None, whole), P(None, whole), P()),
        out_specs=(P(None, whole), P(None, whole)),
        check_vma=False,
    )
```

```python
import jax
import jax.numpy as jnp
from jax import lax
from jax.experimental import pallas as pl
from jax.experimental.pallas import tpu as pltpu
from jax.sharding import Mesh, PartitionSpec as P

PROBES = 16
TILE = 256
TD = 9
BT = 2
MID = TD - 2 * BT
HALO = 2 * BT + 2 * MID
CHUNK = 32
GROUP = 4
ROWS = 24
FIRST = ROWS - PROBES
VMEM = pltpu.MemorySpace.VMEM
SMEM = pltpu.MemorySpace.SMEM
PARTS = ((0, BT), (BT, MID), (TD - BT, BT))


def call(kernel, out_shape, in_specs, scratch=(), aliases=None, flops=0, nbytes=0, limit=10):
    def place(out):
        return pl.BlockSpec(memory_space=getattr(out, "memory_space", VMEM))

    return pl.pallas_call(
        kernel,
        out_shape=out_shape,
        in_specs=in_specs,
        out_specs=jax.tree.map(place, out_shape),
        scratch_shapes=scratch,
        input_output_aliases=aliases or {},
        compiler_params=pltpu.CompilerParams(vmem_limit_bytes=limit << 20),
        cost_estimate=pl.CostEstimate(flops=flops, bytes_accessed=nbytes, transcendentals=0),
    )


def spec(space=VMEM):
    return pl.BlockSpec(memory_space=space)


def f32(*shape):
    return jax.ShapeDtypeStruct(shape, jnp.float32)


def pinned(space, *arrays):
    return tuple(pltpu.with_memory_space_constraint(a, space) for a in arrays)


def pack_kernel(probes, coords, pairs, scales, left, mid, right, pair_out, scale_out, sems):
    copies = [
        pltpu.make_async_copy(pairs, pair_out, sems.at[6]),
        pltpu.make_async_copy(scales, scale_out, sems.at[7]),
    ]
    for i, ((first, count), out) in enumerate(zip(PARTS, (left, mid, right))):
        cols = pl.ds(first * TILE, count * TILE)
        copies.append(pltpu.make_async_copy(probes.at[:, cols], out.at[FIRST:ROWS, :], sems.at[i]))
        copies.append(pltpu.make_async_copy(coords.at[:, cols], out.at[0:3, :], sems.at[3 + i]))
    for copy in copies:
        copy.start()
    for out in (left, mid, right):
        out[3:FIRST, :] = jnp.zeros((FIRST - 3, out.shape[1]), jnp.float32)
    for copy in copies:
        copy.wait()


def make_lists(pairs, rows, cols, counts):
    slots = pairs.shape[1]

    def close(taken, at):
        for i in range(GROUP):
            rows[at, taken + i] = TD
            cols[at, taken + i] = 0
        return (taken + GROUP - 1) // GROUP * GROUP

    def step(j, taken):
        own, halo = taken
        row, code = pairs[0, j], pairs[1, j]
        used = row < TD
        local = used & (code < TD)
        other = used & (code >= TD)
        place = jnp.where(
            code < 2 * TD,
            code - (2 * TD - BT),
            jnp.where(
                code < 3 * TD,
                code - 2 * TD + BT,
                jnp.where(code < 4 * TD, code - 3 * TD + BT, code - 4 * TD + BT + MID),
            ),
        )
        rows[0, own] = row
        cols[0, own] = code
        rows[1, halo] = row
        cols[1, halo] = place
        return own + local.astype(jnp.int32), halo + other.astype(jnp.int32)

    own, halo = lax.fori_loop(0, slots, step, (0, 0), unroll=4)
    counts[0] = close(own, 0)
    counts[1] = close(halo, 1)


def split(values):
    high = values.astype(jnp.bfloat16)
    return high, (values - high.astype(jnp.float32)).astype(jnp.bfloat16)


def put_vectors(values, vecs, at):
    high, low = split(values)
    vecs[at, 0:PROBES, :] = high
    vecs[at, PROBES:, :] = low


def evaluate(near, far, slot, high, low):
    for first in range(0, TILE, CHUNK):
        rows = pl.ds(first, CHUNK)
        for half in range(0, TILE, 128):
            lanes = pl.ds(half, 128)
            dx = near[0, rows, :] - far[0:1, lanes]
            dy = near[1, rows, :] - far[1:2, lanes]
            dz = near[2, rows, :] - far[2:3, lanes]
            dist_sq = dx * dx + dy * dy + dz * dz
            radius = dist_sq * lax.rsqrt(jnp.maximum(dist_sq, 1e-30))
            inside = jnp.maximum(1.0 - radius, 0.0)
            square = inside * inside
            phi = (square * square) * (1.25 - inside)
            top, rest = split(phi)
            high[slot, rows, lanes] = top
            low[slot, rows, lanes] = rest


def dot(vectors, matrix):
    return lax.dot_general(
        vectors, matrix, (((1,), (1,)), ((), ())), preferred_element_type=jnp.float32
    )


def multiply(vecs, source, slot, high, low):
    both = dot(vecs[source], high[slot])
    rest = dot(vecs[source, 0:PROBES, :], low[slot])
    return both[0:PROBES] + both[PROBES:] + rest


def add_group(first, base, rows, cols, vecs, total, high, low):
    sums = [
        (rows[first + i], multiply(vecs, cols[first + i], base + first + i, high, low))
        for i in range(GROUP)
    ]
    for row, value in sums:
        total[row] += value


def first_sweep(base, taken, rows, cols, near, far, vecs, total, high, low):
    def phi(first):
        for i in range(GROUP):
            evaluate(near.at[rows[first + i]], far.at[cols[first + i]], base + first + i, high, low)

    @pl.when(taken > 0)
    def _():
        phi(0)

        def step(k, carry):
            add_group(k * GROUP - GROUP, base, rows, cols, vecs, total, high, low)
            phi(k * GROUP)
            return carry

        lax.fori_loop(1, taken // GROUP, step, 0)
        add_group(taken - GROUP, base, rows, cols, vecs, total, high, low)


def second_sweep(base, taken, rows, cols, vecs, total, high, low):
    def step(k, carry):
        add_group(k * GROUP, base, rows, cols, vecs, total, high, low)
        return carry

    lax.fori_loop(0, taken // GROUP, step, 0)


def own_blocks(refs):
    for (first, count), ref in zip(PARTS, refs):
        for t in range(count):
            yield first + t, ref, pl.ds(t * TILE, TILE)


def halo_blocks(from_left, from_right, below, above):
    at = 0
    for ref, count in ((from_left, BT), (from_right, BT), (below, MID), (above, MID)):
        for t in range(count):
            yield at, ref, pl.ds(t * TILE, TILE)
            at += 1


def phi_own_kernel(
    pairs, left, mid, right, total, high, low, near, rows, cols, counts, far, vecs
):
    make_lists(pairs, rows, cols, counts)
    for t, ref, at in own_blocks((left, mid, right)):
        points = ref[0:FIRST, at]
        far[t] = points
        columns = points.T
        for i in range(3):
            near[t, i] = jnp.broadcast_to(columns[:, i : i + 1], (TILE, 128))
        put_vectors(ref[FIRST:ROWS, at], vecs, t)
    near[TD] = jnp.zeros((3, TILE, 128), jnp.float32)
    total[...] = jnp.zeros_like(total)
    first_sweep(0, counts[0], rows.at[0], cols.at[0], near, far, vecs, total, high, low)


def phi_halo_kernel(
    rows, cols, counts, scales, left, mid, right, from_left, from_right, below, above, part, near, high_in, low_in,
    p_left, p_mid, p_right, high, low, far, vecs, total,
):
    for t, ref, at in halo_blocks(from_left, from_right, below, above):
        far[t] = ref[0:FIRST, at]
        put_vectors(ref[FIRST:ROWS, at], vecs, t)
    total[...] = part[...]
    first_sweep(counts[0], counts[1], rows.at[1], cols.at[1], near, far, vecs, total, high, low)
    outs = {}
    for t, ref, at in own_blocks((p_left, p_mid, p_right)):
        outs[t] = (ref, at)
    for t, ref, at in own_blocks((left, mid, right)):
        out, place = outs[t]
        out[:, place] = scales[0] * (4.0 * total[t] - ref[FIRST:ROWS, at])


def own_kernel(rows, cols, counts, left, mid, right, high, low, total, vecs):
    for t, ref, at in own_blocks((left, mid, right)):
        put_vectors(ref[:, at], vecs, t)
    total[...] = jnp.zeros_like(total)
    second_sweep(0, counts[0], rows.at[0], cols.at[0], vecs, total, high, low)


def halo_kernel(
    rows, cols, counts, scales, r_left, r_mid, r_right, left, mid, right,
    from_left, from_right, below, above, part, high, low, image, dots, vecs, total,
):
    for t, ref, at in halo_blocks(from_left, from_right, below, above):
        put_vectors(ref[:, at], vecs, t)
    total[...] = part[...]
    second_sweep(counts[0], counts[1], rows.at[1], cols.at[1], vecs, total, high, low)
    probes = {t: ref[FIRST:ROWS, at] for t, ref, at in own_blocks((r_left, r_mid, r_right))}
    sums = [jnp.zeros((PROBES, TILE), jnp.float32) for _ in range(5)]
    for t, ref, at in own_blocks((left, mid, right)):
        p = ref[:, at]
        u = scales[0] * (4.0 * total[t] - p)
        r = probes[t]
        image[:, pl.ds(t * TILE, TILE)] = u
        for i, (one, other) in enumerate(((r, r), (r, p), (p, p), (r, u), (p, u))):
            sums[i] = sums[i] + one * other
    lane = lax.broadcasted_iota(jnp.int32, (PROBES, 128), 1)
    probe = lax.broadcasted_iota(jnp.int32, (PROBES, 128), 0)
    line = jnp.zeros((PROBES, 128), jnp.float32)
    for i, value in enumerate(sums):
        line = line + jnp.where(lane == i * PROBES + probe, jnp.sum(value, axis=1, keepdims=True), 0.0)
    dots[...] = jnp.broadcast_to(jnp.sum(line, axis=0, keepdims=True), dots.shape)


def pass_kernel(gathered, out):
    out[...] = jnp.broadcast_to(jnp.sum(gathered[...], axis=0, keepdims=True), out.shape)


def final_kernel(
    gathered, scales, r_left, r_mid, r_right, left, mid, right, image, solution, residual
):
    line = jnp.sum(gathered[...], axis=0, keepdims=True)
    lane = lax.broadcasted_iota(jnp.int32, (PROBES, 128), 1)
    probe = lax.broadcasted_iota(jnp.int32, (PROBES, 128), 0)
    spread = jnp.broadcast_to(line, (PROBES, 128))
    rr, rp, pp, ru, pu = [
        jnp.sum(jnp.where(lane == i * PROBES + probe, spread, 0.0), axis=1, keepdims=True)
        for i in range(5)
    ]
    shift = scales[0] + scales[1]
    first = rr / (shift * rr + rp)
    ratio = rp / rr
    norm = first * first * (pp - rp * ratio)
    turn = norm / rr
    keep = first * ratio + turn
    curve = (
        shift * (norm + turn * norm) + keep * keep * rp - keep * first * (ru + pp) + first * first * pu
    )
    second = norm / curve
    own_r = first + second * keep
    own_p = second * first
    res_r = first * ratio - second * shift * keep
    res_p = second * (shift * first - keep) - first
    res_u = second * first
    probes = {t: ref[FIRST:ROWS, at] for t, ref, at in own_blocks((r_left, r_mid, r_right))}
    for t, ref, at in own_blocks((left, mid, right)):
        cols = pl.ds(t * TILE, TILE)
        r, p = probes[t], ref[:, at]
        solution[:, cols] = own_r * r - own_p * p
        residual[:, cols] = res_r * r + res_p * p + res_u * image[:, cols]


def exchange(left, mid, right):
    lon = ("x", "z")
    depth = ("y", "core")
    up = lambda axes: [(i, i + 1) for i in range(lax.axis_size(axes) - 1)]
    down = lambda axes: [(i + 1, i) for i in range(lax.axis_size(axes) - 1)]
    return (
        lax.ppermute(right, lon, up(lon)),
        lax.ppermute(left, lon, down(lon)),
        lax.ppermute(mid, depth, up(depth)),
        lax.ppermute(mid, depth, down(depth)),
    )


def sweeps(probes, coords, pairs, scales, first_exchange, second_exchange, copies):
    slots = pairs.shape[1]
    width = probes.shape[1]
    pair_flops = 40 * TILE * TILE * slots // 2
    stored = (slots + 2 * GROUP, TILE, TILE)
    kept = (pltpu.VMEM(stored, jnp.bfloat16), pltpu.VMEM(stored, jnp.bfloat16))
    lists = (
        pltpu.SMEM((2, slots + GROUP), jnp.int32),
        pltpu.SMEM((2, slots + GROUP), jnp.int32),
        pltpu.SMEM((2,), jnp.int32),
    )
    pieces = lambda rows: tuple(f32(rows, count * TILE) for _, count in PARTS)
    total = (TD + 1, PROBES, TILE)

    *packed, pairs, scales = call(
        pack_kernel,
        (*pieces(ROWS), pltpu.SMEM(pairs.shape, jnp.int32), pltpu.SMEM(scales.shape, jnp.float32)),
        [spec(pl.ANY)] * 4,
        scratch=[pltpu.SemaphoreType.DMA((8,))],
        nbytes=8 * ROWS * width,
    )(*pinned(pltpu.MemorySpace.HBM, probes, coords, pairs, scales))
    halo = first_exchange(*packed)
    part, high, low, near, *lists = call(
        phi_own_kernel,
        (f32(*total), *kept, pltpu.VMEM((TD + 1, 3, TILE, 128), jnp.float32), *lists),
        [spec(SMEM)] + [spec()] * 3,
        scratch=[
            pltpu.VMEM((TD, FIRST, TILE), jnp.float32),
            pltpu.VMEM((TD, 2 * PROBES, TILE), jnp.bfloat16),
        ],
        flops=pair_flops,
        nbytes=1 << 20,
    )(*pinned(SMEM, pairs), *packed)
    lists = pinned(SMEM, *lists)
    (scales,) = pinned(SMEM, scales)
    *image, high, low = call(
        phi_halo_kernel,
        (*pieces(PROBES), *kept),
        [spec(SMEM)] * 4 + [spec()] * 11,
        scratch=[
            pltpu.VMEM((HALO, FIRST, TILE), jnp.float32),
            pltpu.VMEM((HALO, 2 * PROBES, TILE), jnp.bfloat16),
            pltpu.VMEM(total, jnp.float32),
        ],
        aliases={13: 3, 14: 4},
        flops=pair_flops,
        nbytes=1 << 20,
    )(*lists, scales, *packed, *halo, part, *pinned(VMEM, near, high, low))
    halo = second_exchange(*image)
    part = call(
        own_kernel,
        f32(*total),
        [spec(SMEM)] * 3 + [spec()] * 5,
        scratch=[pltpu.VMEM((TD, 2 * PROBES, TILE), jnp.bfloat16)],
        flops=pair_flops // 2,
        nbytes=1 << 20,
    )(*lists, *image, *pinned(VMEM, high, low))
    far_image, dots = call(
        halo_kernel,
        (f32(PROBES, width), f32(copies, 128)),
        [spec(SMEM)] * 4 + [spec()] * 13,
        scratch=[
            pltpu.VMEM((HALO, 2 * PROBES, TILE), jnp.bfloat16),
            pltpu.VMEM(total, jnp.float32),
        ],
        flops=pair_flops // 2,
        nbytes=1 << 20,
    )(*lists, scales, *packed, *image, *halo, part, *pinned(VMEM, high, low))
    return scales, packed, image, far_image, dots


def body(probes, coords, pairs, scales):
    scales, packed, image, far_image, dots = sweeps(
        probes, coords, pairs, scales, exchange, exchange, lax.axis_size(("core", "z"))
    )

    def swap(rows, axes):
        return lax.all_to_all(rows[:, None, :], axes, 0, 0, tiled=True)[:, 0, :]

    rows = swap(dots, ("core", "z"))
    rows = call(pass_kernel, f32(lax.axis_size(("y", "x")), 128), [spec()])(rows)
    rows = swap(rows, ("y", "x"))
    return call(final_kernel, (f32(*probes.shape),) * 2, [spec(), spec(SMEM)] + [spec()] * 7)(
        rows, scales, *packed, *image, far_image
    )


def solution(mesh):
    shape = mesh.devices.shape
    cut = Mesh(mesh.devices.reshape(shape[0] // 2, 2, 4, shape[1] // 4), ("y", "core", "x", "z"))
    whole = ("y", "core", "x", "z")
    return jax.shard_map(
        body,
        mesh=cut,
        in_specs=(P(None, whole), P(None, whole), P(None, whole), P()),
        out_specs=(P(None, whole), P(None, whole)),
        check_vma=False,
    )
```
